1024 devices in a mesh: segment: 8 (over x, core), dp: 32 (over z, y_lo), seq: 4 (over y_hi).
Axes of the slice: x: 4, y: 8 (y_hi: 4, y_lo: 2; y = y_hi * 2 + y_lo), z: 16, core: 2. Of those that a mesh axis runs over, the one named last changes fastest.
Arguments:
- query_in: bfloat16 [256, 512, 1536], P(('segment', 'dp'), 'seq'), may hold values from -6 to 6
- key_in: bfloat16 [256, 512, 1536], P(('segment', 'dp'), 'seq'), may hold values from -6 to 6
- value_in: bfloat16 [256, 512, 1536], P(('segment', 'dp'), 'seq'), may hold values from -6 to 6
- latent_now: bfloat16 [256, 512, 1536], P(('segment', 'dp'), 'seq'), may hold values from -6 to 6
- latent_next: bfloat16 [256, 512, 1536], P(('segment', 'dp'), 'seq'), may hold values from -6 to 6
- norm_gains: float32 [2, 128], replicated, may hold values from 0.1 to 1.9
- rewards: float32 [256], replicated, may hold values from -2 to 2
- step_index: int32 [256], replicated, may hold values from 0 to 15
- token_count: int32 [256], replicated, may hold values from 128 to 512, as said below
Outputs:
- grad_query: bfloat16 [256, 512, 1536], P(('segment', 'dp'), None, 'seq')
- grad_key: bfloat16 [256, 512, 1536], P(('segment', 'dp'), None, 'seq')
- grad_value: bfloat16 [256, 512, 1536], P(('segment', 'dp'), None, 'seq')
- gain_grads: float32 [2, 128], replicated
The draws below stay inside these ranges and needn't reach their ends.
Inputs may be any that keep to these rules, and one draw needn't show every extreme that they name: `token_count`: valid tokens of each video; some video has exactly 512.
All inputs are finite; a program needn't handle non-finite values.
Results may differ from the reference program's by a relative error of at most 0.018.
Values may be sent and summed in bfloat16 or wider, within the bound.
No kernel may reach another device: no remote copies, remote signals or barrier semaphores. Data moves between devices by JAX's collectives and lax.ppermute only.
A program may use at most 32 MiB of HBM per device.

```python
import jax
import jax.numpy as jnp
from jax import lax

HEADS = 12
HEAD = 128
D = 1536
SEQ = 512
STEPS = 16
GROUP = 16
VIDEOS = 256
GROUPS = 16
N_DP = 32


def draw_rewards(key, part):
    scale_key = jax.random.fold_in(key, 11)
    base_key = jax.random.fold_in(key, 12)
    scales = jnp.exp(jax.random.uniform(scale_key, (GROUPS,), jnp.float32, jnp.log(0.05), jnp.log(2.0)))
    member = jnp.arange(VIDEOS) // GROUP
    base = jax.random.uniform(base_key, (VIDEOS,), jnp.float32, -1.0, 1.0)
    return base * scales[member]


def draw_token_count(key, part):
    count_key = jax.random.fold_in(key, 21)
    full_key = jax.random.fold_in(key, 22)
    counts = jax.random.randint(count_key, (VIDEOS,), SEQ // 4, SEQ + 1)
    full = jax.random.randint(full_key, (), 0, VIDEOS)
    return jnp.where(jnp.arange(VIDEOS) == full, SEQ, counts).astype(jnp.int32)


def touch_ends(values, own_key, smallest, top_value):
    longest = values.shape.index(max(values.shape))
    spots = []
    for shift in (0, 1):
        where = [jax.random.randint(jax.random.fold_in(own_key, axis), (), 0, length) for axis, length in enumerate(values.shape)]
        where[longest] = (where[longest] + shift) % values.shape[longest]
        spots.append(tuple(where))
    return values.at[spots[0]].set(smallest).at[spots[1]].set(top_value)


def level_of(stream_key, dims, shards, smallest, top_value):
    level = 1.0
    for axis_at, shards_of in shards:
        heights = jax.random.uniform(jax.random.fold_in(jax.random.fold_in(stream_key, 6), axis_at), (shards_of,), jnp.float32, smallest / len(shards), top_value / len(shards))
        level = level * jnp.repeat(jnp.exp(heights), dims[axis_at] // shards_of).reshape((-1,) + (1,) * (len(dims) - 1 - axis_at))
    return level


def normal_values(stream_key, dims, deviation, most, pieces=(), dtype=jnp.bfloat16):
    factor_of = level_of(stream_key, dims, pieces, -0.22, 0.18) if pieces else 1.0
    array = jax.random.normal(stream_key, dims, jnp.float32) * deviation * factor_of
    return jnp.minimum(jnp.maximum(array, -most), most).astype(dtype)


def setup_inputs(seed: int = 0) -> dict:
    key_of = jax.random.split(jax.random.key(seed), 10)
    return {
        "query_in": normal_values(key_of[0], (VIDEOS, SEQ, D), 1.0, 6.0, ((0, 256), (1, 4))),
        "key_in": normal_values(key_of[1], (VIDEOS, SEQ, D), 1.0, 6.0, ((0, 256), (1, 4))),
        "value_in": normal_values(key_of[2], (VIDEOS, SEQ, D), 1.0, 6.0, ((0, 256), (1, 4))),
        "latent_now": normal_values(key_of[3], (VIDEOS, SEQ, D), 1.0, 6.0, ((0, 256), (1, 4))),
        "latent_next": normal_values(key_of[4], (VIDEOS, SEQ, D), 1.0, 6.0, ((0, 256), (1, 4))),
        "norm_gains": jnp.clip(1.0 + 0.18 * jax.random.normal(key_of[5], (2, HEAD), jnp.float32), 0.1, 1.9),
        "rewards": draw_rewards(jax.random.fold_in(key_of[9], 71), 0),
        "step_index": touch_ends(jax.random.randint(key_of[7], (VIDEOS,), 0, STEPS), jax.random.fold_in(key_of[7], 1), 0, STEPS - 1).astype(jnp.int32),
        "token_count": draw_token_count(jax.random.fold_in(key_of[9], 71), 0),
    }


def head_norm(values, gain):
    wide = values.astype(jnp.float32)
    scaled = wide * lax.rsqrt(lax.optimization_barrier(jnp.mean(wide * wide, axis=-1, keepdims=True)) + 1e-06)
    return (scaled * gain).astype(jnp.bfloat16)

def head_grads(query, keys, values, now_rows, next_rows, gains, advantage, delta, count):
    length = query.shape[0]
    keep = jnp.arange(length) < count

    def forward(q_in, k_in, v_in, gains_in):
        q_rows = head_norm(q_in, gains_in[0])
        k_rows = head_norm(k_in, gains_in[1])
        scores = jnp.dot(q_rows, k_rows.T, preferred_element_type=jnp.float32) / jnp.sqrt(jnp.float32(q_in.shape[1]))
        scores = jnp.where(keep[None, :], scores, jnp.float32(-1e+30))
        weights = jax.nn.softmax(scores, axis=-1).astype(jnp.bfloat16)
        return jnp.dot(weights, v_in, preferred_element_type=jnp.float32)
    velocity, pull = jax.vjp(forward, query, keys, values, gains)
    mean_next = now_rows.astype(jnp.float32) - delta * velocity
    cotangent = jnp.where(keep[:, None], advantage * (next_rows.astype(jnp.float32) - mean_next), jnp.float32(0.0))
    return pull(cotangent)

def group_advantage(rewards):
    total = rewards.shape[0]
    member = (jnp.arange(total)[:, None] // GROUP == jnp.arange(total // GROUP)[None, :]).astype(jnp.float32)
    means = jnp.dot(rewards, member) / GROUP
    mean_rows = jnp.dot(member, means)
    spreads = jnp.sqrt(jnp.dot((rewards - mean_rows) ** 2, member) / GROUP)
    return (rewards - mean_rows) / jnp.maximum(jnp.dot(member, spreads), jnp.float32(0.25))

def step_sigma(index):
    level = 1.0 - index.astype(jnp.float32) / STEPS
    return 7.0 * level / (1.0 + 6.0 * level)

def reference(query_in, key_in, value_in, latent_now, latent_next, norm_gains, rewards, step_index, token_count):
    advantage = jnp.roll(group_advantage(rewards), N_DP, axis=0)
    delta = jnp.roll(step_sigma(step_index) - step_sigma(step_index + 1), N_DP, axis=0)
    counts = jnp.roll(token_count, N_DP, axis=0)
    arrays = tuple((jnp.roll(a, N_DP, axis=0).reshape(VIDEOS, SEQ, HEADS, HEAD) for a in (query_in, key_in, value_in, latent_now, latent_next)))

    def one_video(items):
        q_all, k_all, v_all, now_all, next_all, adv, dlt, cnt = items
        moved = tuple((jnp.moveaxis(a, 1, 0) for a in (q_all, k_all, v_all, now_all, next_all)))
        grads = jax.vmap(lambda a, b, c, d, e: head_grads(a, b, c, d, e, norm_gains, adv, dlt, cnt))(*moved)
        return (jnp.moveaxis(grads[0], 0, 1), jnp.moveaxis(grads[1], 0, 1), jnp.moveaxis(grads[2], 0, 1), lax.optimization_barrier(jnp.sum(grads[3], axis=0)))
    dq, dk, dv, dg = lax.map(one_video, arrays + (advantage, delta, counts))
    gain_grads = lax.optimization_barrier(jnp.sum(dg, axis=0)) / VIDEOS
    return (dq.reshape(VIDEOS, SEQ, D).astype(jnp.bfloat16), dk.reshape(VIDEOS, SEQ, D).astype(jnp.bfloat16), dv.reshape(VIDEOS, SEQ, D).astype(jnp.bfloat16), gain_grads)
```

```python
import functools
import math

import jax
import jax.numpy as jnp
from jax import lax
from jax.experimental import pallas as pl
from jax.experimental.pallas import tpu as pltpu
from jax.sharding import PartitionSpec as P

HEAD = 128
STEPS = 16
GROUP = 16
ORDER = (2, 1, 3)


def chunks_of(heads):
    return ((0, heads - 1), (heads - 1, 1)) if heads > 1 else ((0, 1),)


def moved(value, step):
    segments, shards = lax.axis_size("segment"), lax.axis_size("seq")
    pairs = [
        (s * shards + q, (s + 1) % segments * shards + (q + step) % shards)
        for s in range(segments)
        for q in range(shards)
    ]
    return lax.ppermute(value, ("segment", "seq"), pairs)


def pack_kernel(plan, shards, where, query, key, value, now, following, *outs):
    mine = where[0]
    width = query.shape[2] // shards
    for (step, first, heads), out in zip(plan, outs):
        place = lax.rem(mine + step, shards) * width + first * HEAD
        cols = pl.ds(pl.multiple_of(place, HEAD), heads * HEAD)
        out[0] = query[0, :, cols]
        out[1] = key[0, :, cols]
        out[2] = value[0, :, cols]
        out[3] = (
            following[0, :, cols].astype(jnp.float32) - now[0, :, cols].astype(jnp.float32)
        ).astype(jnp.bfloat16)


def pack(plan, shards, where, arrays):
    rows = arrays[0].shape[1]
    return pl.pallas_call(
        functools.partial(pack_kernel, plan, shards),
        out_shape=[
            jax.ShapeDtypeStruct((4, rows, heads * HEAD), jnp.bfloat16) for _, _, heads in plan
        ],
        in_specs=[pl.BlockSpec(memory_space=pltpu.SMEM)]
        + [pl.BlockSpec(memory_space=pltpu.VMEM)] * 5,
        out_specs=[pl.BlockSpec(memory_space=pltpu.VMEM)] * len(plan),
        cost_estimate=pl.CostEstimate(flops=1, bytes_accessed=2 << 20, transcendentals=0),
        name="pack",
    )(where, *arrays)


def slot_scalars(source, rewards, steps, counts):
    total = rewards.shape[1]
    lane = lax.broadcasted_iota(jnp.int32, (1, total), 1)
    of_group = (lane // GROUP) == (source // GROUP)
    of_slot = lane == source

    def picked(which, row):
        return jnp.sum(jnp.where(which, row, jnp.zeros_like(row)), axis=1, keepdims=True)

    mean = picked(of_group, rewards) / GROUP
    spread = jnp.sqrt(picked(of_group, (rewards - mean) ** 2) / GROUP)
    advantage = (picked(of_slot, rewards) - mean) / jnp.maximum(spread, jnp.float32(0.25))
    index = picked(of_slot, steps.astype(jnp.float32))

    def sigma(k):
        level = 1.0 - k / STEPS
        return 7.0 * level / (1.0 + 6.0 * level)

    delta = sigma(index) - sigma(index + 1.0)
    count = picked(of_slot, counts.astype(jnp.float32))
    return advantage, delta, count


def dot(a, b, dims):
    return lax.dot_general(a, b, (dims, ((), ())), preferred_element_type=jnp.float32)


def attend_kernel(
    first, shards, where, rewards, steps, counts, gains, prior, b0, b1, b2, b3, *rest
):
    dq_ref, dk_ref, dv_ref, dg_ref, e_ref, ds_ref = rest[-6:]
    mine, source = where[0], where[1]
    advantage, delta, count = slot_scalars(source, rewards[...], steps[...], counts[...])
    blocks = (b0, b1, b2, b3)
    rows = b0.shape[1]
    gain_q, gain_k = gains[0:1, :], gains[1:2, :]
    inv_root = 1.0 / math.sqrt(HEAD)

    starts, valid = [], []
    for d in range(shards):
        start = lax.rem(mine - d + shards, shards) * rows
        starts.append(pl.multiple_of(start, rows))
        token = lax.broadcasted_iota(jnp.int32, (rows, HEAD), 0) + start
        valid.append(token.astype(jnp.float32) < count)

    def normed(block, at, gain):
        wide = block[at].astype(jnp.float32)
        scale = lax.rsqrt(jnp.mean(wide * wide, axis=-1, keepdims=True) + 1e-06)
        return wide * scale, scale, gain

    q_hat, q_scale, q_rows, k_hat, k_scale, k_rows, v_rows = [], [], [], [], [], [], []
    for d, block in enumerate(blocks):
        hat, scale, _ = normed(block, 0, gain_q)
        q_hat.append(hat), q_scale.append(scale)
        q_rows.append((hat * gain_q).astype(jnp.bfloat16))
        hat, scale, _ = normed(block, 1, gain_k)
        k_hat.append(hat), k_scale.append(scale)
        k_rows.append(jnp.where(valid[d], hat * gain_k, 0.0).astype(jnp.bfloat16))
        v_rows.append(jnp.where(valid[d], block[2].astype(jnp.float32), 0.0).astype(jnp.bfloat16))
    keys = jnp.concatenate(k_rows, axis=0)
    values = jnp.concatenate(v_rows, axis=0)
    keep = jnp.concatenate([jnp.where(m, 1.0, 0.0).astype(jnp.bfloat16) for m in valid], axis=0)
    values_keep = jnp.concatenate([values, keep], axis=1)

    pulls, grad_gq = [], jnp.zeros((1, HEAD), jnp.float32)
    for d, block in enumerate(blocks):
        here = pl.ds(d * rows, rows)
        scores = dot(q_rows[d], keys, ((1,), (1,)))
        e = jnp.exp2(scores * (inv_root * math.log2(math.e)))
        e_low = e.astype(jnp.bfloat16)
        e_ref[here, :] = e_low
        both = dot(e_low, values_keep, ((1,), (0,)))
        share = 1.0 / both[:, HEAD:]
        velocity = both[:, :HEAD] * share
        pull = jnp.where(
            valid[d], advantage * (block[3].astype(jnp.float32) + delta * velocity), 0.0
        )
        pull = (pull * share).astype(jnp.bfloat16)
        pulls.append(pull)
        level = jnp.sum(pull.astype(jnp.float32) * velocity, axis=-1, keepdims=True)
        d_weights = dot(pull, values, ((1,), (1,)))
        ds = (e * (d_weights - level)).astype(jnp.bfloat16)
        ds_ref[here, :] = ds
        d_rows = dot(ds, keys, ((1,), (0,))) * inv_root
        grad_gq += jnp.sum(d_rows * q_hat[d], axis=0, keepdims=True)
        inner = d_rows * gain_q
        inner = inner - q_hat[d] * jnp.mean(inner * q_hat[d], axis=-1, keepdims=True)
        dq_ref[0, pl.ds(starts[d], rows), :] = (inner * q_scale[d]).astype(jnp.bfloat16)

    d_keys = dot(ds_ref[...], jnp.concatenate(q_rows, axis=0), ((0,), (0,))) * inv_root
    grad_gk = jnp.zeros((1, HEAD), jnp.float32)
    for d in range(shards):
        d_rows = jnp.where(valid[d], d_keys[d * rows : (d + 1) * rows], 0.0)
        grad_gk += jnp.sum(d_rows * k_hat[d], axis=0, keepdims=True)
        inner = d_rows * gain_k
        inner = inner - k_hat[d] * jnp.mean(inner * k_hat[d], axis=-1, keepdims=True)
        dk_ref[0, pl.ds(starts[d], rows), :] = (inner * k_scale[d]).astype(jnp.bfloat16)
    d_values = dot(e_ref[...], jnp.concatenate(pulls, axis=0), ((0,), (0,)))
    for d in range(shards):
        d_rows = jnp.where(valid[d], d_values[d * rows : (d + 1) * rows], 0.0)
        dv_ref[0, pl.ds(starts[d], rows), :] = d_rows.astype(jnp.bfloat16)

    both_gains = jnp.concatenate([grad_gq, grad_gk], axis=0)[None]

    @pl.when(pl.program_id(0) == 0)
    def _():
        dg_ref[...] = jnp.broadcast_to(prior[0:1] + both_gains, dg_ref.shape)

    @pl.when(pl.program_id(0) > 0)
    def _():
        dg_ref[...] += jnp.broadcast_to(both_gains, dg_ref.shape)


def attend(first, heads, heads_local, copies, where, facts, gains, prior, blocks, grads):
    shards = len(blocks)
    rows = blocks[0].shape[1]
    length = rows * shards
    whole = pl.BlockSpec(memory_space=pltpu.VMEM)
    block_specs = []
    for block in blocks:
        shift = first if block.shape[2] > heads * HEAD else 0
        block_specs.append(
            pl.BlockSpec((4, rows, HEAD), functools.partial(lambda s, h: (0, 0, s + h), shift))
        )
    grad_spec = pl.BlockSpec((1, length, HEAD), lambda h: (0, 0, first + h))
    grad_shape = jax.ShapeDtypeStruct((1, length, heads_local * HEAD), jnp.bfloat16)
    out = pl.pallas_call(
        functools.partial(attend_kernel, first, shards),
        grid=(heads,),
        out_shape=[grad_shape] * 3 + [jax.ShapeDtypeStruct((copies, 2, HEAD), jnp.float32)],
        in_specs=[pl.BlockSpec(memory_space=pltpu.SMEM)]
        + [whole] * 5
        + block_specs
        + [pl.BlockSpec(memory_space=pl.ANY)] * len(grads),
        out_specs=[grad_spec] * 3 + [pl.BlockSpec((copies, 2, HEAD), lambda h: (0, 0, 0))],
        scratch_shapes=[pltpu.VMEM((length, length), jnp.bfloat16)] * 2,
        input_output_aliases={6 + shards + i: i for i in range(len(grads))},
        compiler_params=pltpu.CompilerParams(dimension_semantics=("arbitrary",)),
        cost_estimate=pl.CostEstimate(
            flops=heads * 12 * length * length * HEAD,
            bytes_accessed=heads * 8 * length * HEAD * 2,
            transcendentals=heads * length * length,
        ),
        name="attend",
    )(where, *facts, gains, prior, *blocks, *grads)
    return out[:3], out[3]


def gathered_sum(spread, axes):
    return jnp.sum(lax.all_to_all(spread, axes, 0, 0, tiled=True), axis=0)


def body(
    query_in,
    key_in,
    value_in,
    latent_now,
    latent_next,
    norm_gains,
    rewards,
    step_index,
    token_count,
):
    segments = lax.axis_size("segment")
    replicas = lax.axis_size("dp")
    shards = lax.axis_size("seq")
    source = (lax.axis_index("segment") + segments - 1) % segments * replicas + lax.axis_index("dp")
    where = jnp.stack([lax.axis_index("seq"), source]).astype(jnp.int32)
    heads_local = query_in.shape[2] // HEAD // shards
    chunks = chunks_of(heads_local)

    plan = []
    for c, (first, heads) in enumerate(chunks):
        plan += [(step, first, heads) for step in ORDER]
        if c == 0:
            plan.append((0, 0, heads_local))
    sent = pack(plan, shards, where, (query_in, key_in, value_in, latent_now, latent_next))
    arrived = {(step, first): moved(a, step) for (step, first, _), a in zip(plan, sent)}

    facts = tuple(a[None] for a in (rewards, step_index, token_count))
    grads, partial = (), jnp.zeros((1, 2, HEAD), jnp.float32)
    for c, (first, heads) in enumerate(chunks):
        blocks = [arrived[0, 0]] + [arrived[step, first] for step in range(1, shards)]
        copies = replicas if c == len(chunks) - 1 else 1
        grads, partial = attend(
            first, heads, heads_local, copies, where, facts, norm_gains, partial, blocks, grads
        )
    by_dp = gathered_sum(partial, "dp")
    others = segments * shards
    total = gathered_sum(jnp.broadcast_to(by_dp[None], (others, 2, HEAD)), ("segment", "seq"))
    return (*grads, total / (segments * replicas))


def solution(mesh):
    rows = P(("segment", "dp"), "seq", None)
    return jax.shard_map(
        body,
        mesh=mesh,
        in_specs=(rows,) * 5 + (P(),) * 4,
        out_specs=(P(("segment", "dp"), None, "seq"),) * 3 + (P(),),
        check_vma=False,
    )
```

```python
import functools
import math

import jax
import jax.numpy as jnp
from jax import lax
from jax.experimental import pallas as pl
from jax.experimental.pallas import tpu as pltpu
from jax.sharding import PartitionSpec as P

HEAD = 128
STEPS = 16
GROUP = 16
STAY, SAME, FAR, BACK = (0, 0), (-1, 1), (2, 2), (1, -1)


def chunks_of(heads):
    return ((0, heads - 1), (heads - 1, 1)) if heads > 1 else ((0, 1),)


def step_at(steps, replica, shards):
    return jnp.where(replica % 2 == 0, steps[0] % shards, steps[1] % shards)


def moved(value, steps):
    segments, replicas, shards = (lax.axis_size(a) for a in ("segment", "dp", "seq"))
    pairs = []
    for s in range(segments):
        for r in range(replicas):
            for q in range(shards):
                to = (q + steps[r % 2]) % shards
                pairs.append(
                    ((s * replicas + r) * shards + q, ((s + 1) % segments * replicas + r) * shards + to)
                )
    return lax.ppermute(value, ("segment", "dp", "seq"), pairs)


def pack_kernel(plan, shards, query, key, value, now, following, *rest):
    outs, (now_ref, next_ref, sems) = rest[: len(plan)], rest[len(plan) :]
    mine, replica = lax.axis_index("seq"), lax.axis_index("dp")
    width = query.shape[2] // shards
    late = [
        pltpu.make_async_copy(now.at[0], now_ref, sems.at[0]),
        pltpu.make_async_copy(following.at[0], next_ref, sems.at[1]),
    ]
    for copy in late:
        copy.start()
    places, copies = [], []
    for n, ((steps, first, heads), out) in enumerate(zip(plan, outs)):
        place = lax.rem(mine + step_at(steps, replica, shards), shards) * width + first * HEAD
        cols = pl.ds(pl.multiple_of(place, HEAD), heads * HEAD)
        places.append(cols)
        for at, array in enumerate((query, key, value)):
            copy = pltpu.make_async_copy(array.at[0, :, cols], out.at[at], sems.at[2 + 3 * n + at])
            copy.start()
            copies.append(copy)
    for copy in late:
        copy.wait()
    for cols, out in zip(places, outs):
        out[3] = (
            next_ref[:, cols].astype(jnp.float32) - now_ref[:, cols].astype(jnp.float32)
        ).astype(jnp.bfloat16)
    for copy in copies:
        copy.wait()


def pack(plan, shards, arrays):
    _, rows, width = arrays[0].shape
    return pl.pallas_call(
        functools.partial(pack_kernel, plan, shards),
        out_shape=[pltpu.VMEM((4, rows, heads * HEAD), jnp.bfloat16) for _, _, heads in plan],
        in_specs=[pl.BlockSpec(memory_space=pl.ANY)] * 5,
        out_specs=[pl.BlockSpec(memory_space=pltpu.VMEM)] * len(plan),
        scratch_shapes=[pltpu.VMEM((rows, width), jnp.bfloat16)] * 2
        + [pltpu.SemaphoreType.DMA((2 + 3 * len(plan),))],
        cost_estimate=pl.CostEstimate(flops=1, bytes_accessed=2 << 20, transcendentals=0),
        name="pack",
    )(*arrays)


def slot_scalars(source, rewards, steps, counts):
    total = rewards.shape[1]
    lane = lax.broadcasted_iota(jnp.int32, (1, total), 1)
    of_group = (lane // GROUP) == (source // GROUP)
    of_slot = lane == source

    def picked(which, row):
        return jnp.sum(jnp.where(which, row, jnp.zeros_like(row)), axis=1, keepdims=True)

    mean = picked(of_group, rewards) / GROUP
    spread = jnp.sqrt(picked(of_group, (rewards - mean) ** 2) / GROUP)
    advantage = (picked(of_slot, rewards) - mean) / jnp.maximum(spread, jnp.float32(0.25))
    index = picked(of_slot, steps.astype(jnp.float32))

    def sigma(k):
        level = 1.0 - k / STEPS
        return 7.0 * level / (1.0 + 6.0 * level)

    delta = sigma(index) - sigma(index + 1.0)
    count = picked(of_slot, counts.astype(jnp.float32))
    return advantage, delta, count


def dot(a, b, dims):
    return lax.dot_general(a, b, (dims, ((), ())), preferred_element_type=jnp.float32)


def attend_kernel(
    first, places, where, rewards, steps, counts, gains, prior, b0, b1, b2, b3, *rest
):
    dq_hbm, dk_hbm, dv_hbm, dg_ref, dq_ref, dk_ref, dv_ref, e_ref, ds_ref, sems = rest[-10:]
    mine, replica, source = where[0], where[1], where[2]
    facts = slot_scalars(source, rewards[...], steps[...], counts[...])
    blocks = (b0, b1, b2, b3)
    shards, rows = len(blocks), b0.shape[1]
    heads = dq_ref.shape[1] // HEAD
    starts, valid = [], []
    for place in places:
        step = step_at(place, replica, shards)
        start = lax.rem(mine - step + shards, shards) * rows
        starts.append(pl.multiple_of(start, rows))
        token = lax.broadcasted_iota(jnp.int32, (rows, HEAD), 0) + start
        valid.append(token.astype(jnp.float32) < facts[2])

    copies = []

    def give(kind, staged, hbm, h):
        cols = pl.ds(h * HEAD, HEAD)
        copy = pltpu.make_async_copy(
            staged.at[:, cols],
            hbm.at[0, :, pl.ds((first + h) * HEAD, HEAD)],
            sems.at[3 * h + kind],
        )
        copy.start()
        copies.append(copy)

    total = prior[0:1]
    for h in range(heads):
        total = total + one_head(
            h, first, blocks, starts, valid, facts, gains, dq_ref, dk_ref, dv_ref, e_ref, ds_ref
        )
        for kind, (staged, hbm) in enumerate(((dq_ref, dq_hbm), (dk_ref, dk_hbm), (dv_ref, dv_hbm))):
            give(kind, staged, hbm, h)
    dg_ref[...] = jnp.broadcast_to(total, dg_ref.shape)
    for copy in copies:
        copy.wait()


def one_head(h, first, blocks, starts, valid, facts, gains, dq_ref, dk_ref, dv_ref, e_ref, ds_ref):
    advantage, delta, _ = facts
    shards, rows = len(blocks), blocks[0].shape[1]
    cols = slice(h * HEAD, (h + 1) * HEAD)
    gain_q, gain_k = gains[0:1, :], gains[1:2, :]
    inv_root = 1.0 / math.sqrt(HEAD)

    def part(block, at):
        skip = first * HEAD if block.shape[2] > dq_ref.shape[1] else 0
        return block[at, :, skip + h * HEAD : skip + (h + 1) * HEAD]

    def normed(block, at):
        wide = part(block, at).astype(jnp.float32)
        scale = lax.rsqrt(jnp.mean(wide * wide, axis=-1, keepdims=True) + 1e-06)
        return wide * scale, scale

    q_hat, q_scale, q_rows, k_hat, k_scale, k_rows, v_rows = [], [], [], [], [], [], []
    for d, block in enumerate(blocks):
        hat, scale = normed(block, 0)
        q_hat.append(hat), q_scale.append(scale)
        q_rows.append((hat * gain_q).astype(jnp.bfloat16))
        hat, scale = normed(block, 1)
        k_hat.append(hat), k_scale.append(scale)
        k_rows.append(jnp.where(valid[d], hat * gain_k, 0.0).astype(jnp.bfloat16))
        v_rows.append(jnp.where(valid[d], part(block, 2).astype(jnp.float32), 0.0).astype(jnp.bfloat16))
    keys = jnp.concatenate(k_rows, axis=0)
    values = jnp.concatenate(v_rows, axis=0)
    keep = jnp.concatenate([jnp.where(m, 1.0, 0.0).astype(jnp.bfloat16) for m in valid], axis=0)
    values_keep = jnp.concatenate([values, keep], axis=1)

    pulls, grad_gq = [], jnp.zeros((1, HEAD), jnp.float32)
    for d, block in enumerate(blocks):
        here = pl.ds(d * rows, rows)
        scores = dot(q_rows[d], keys, ((1,), (1,)))
        e = jnp.exp2(scores * (inv_root * math.log2(math.e)))
        e_low = e.astype(jnp.bfloat16)
        e_ref[here, :] = e_low
        both = dot(e_low, values_keep, ((1,), (0,)))
        share = 1.0 / both[:, HEAD:]
        velocity = both[:, :HEAD] * share
        pull = jnp.where(
            valid[d], advantage * (part(block, 3).astype(jnp.float32) + delta * velocity), 0.0
        )
        pull = (pull * share).astype(jnp.bfloat16)
        pulls.append(pull)
        level = jnp.sum(pull.astype(jnp.float32) * velocity, axis=-1, keepdims=True)
        d_weights = dot(pull, values, ((1,), (1,)))
        ds = (e * (d_weights - level)).astype(jnp.bfloat16)
        ds_ref[here, :] = ds
        d_rows = dot(ds, keys, ((1,), (0,))) * inv_root
        grad_gq += jnp.sum(d_rows * q_hat[d], axis=0, keepdims=True)
        inner = d_rows * gain_q
        inner = inner - q_hat[d] * jnp.mean(inner * q_hat[d], axis=-1, keepdims=True)
        dq_ref[pl.ds(starts[d], rows), cols] = (inner * q_scale[d]).astype(jnp.bfloat16)

    d_keys = dot(ds_ref[...], jnp.concatenate(q_rows, axis=0), ((0,), (0,))) * inv_root
    grad_gk = jnp.zeros((1, HEAD), jnp.float32)
    for d in range(shards):
        d_rows = jnp.where(valid[d], d_keys[d * rows : (d + 1) * rows], 0.0)
        grad_gk += jnp.sum(d_rows * k_hat[d], axis=0, keepdims=True)
        inner = d_rows * gain_k
        inner = inner - k_hat[d] * jnp.mean(inner * k_hat[d], axis=-1, keepdims=True)
        dk_ref[pl.ds(starts[d], rows), cols] = (inner * k_scale[d]).astype(jnp.bfloat16)
    d_values = dot(e_ref[...], jnp.concatenate(pulls, axis=0), ((0,), (0,)))
    for d in range(shards):
        d_rows = jnp.where(valid[d], d_values[d * rows : (d + 1) * rows], 0.0)
        dv_ref[pl.ds(starts[d], rows), cols] = d_rows.astype(jnp.bfloat16)
    return jnp.concatenate([grad_gq, grad_gk], axis=0)[None]


def in_vmem(array):
    return pltpu.with_memory_space_constraint(array, pltpu.VMEM)


def attend(first, heads, heads_local, copies, places, where, facts, gains, prior, blocks, grads):
    shards = len(blocks)
    length = blocks[0].shape[1] * shards
    whole, anywhere = pl.BlockSpec(memory_space=pltpu.VMEM), pl.BlockSpec(memory_space=pl.ANY)
    grad_shape = jax.ShapeDtypeStruct((1, length, heads_local * HEAD), jnp.bfloat16)
    out = pl.pallas_call(
        functools.partial(attend_kernel, first, places),
        out_shape=[grad_shape] * 3 + [jax.ShapeDtypeStruct((copies, 2, HEAD), jnp.float32)],
        in_specs=[pl.BlockSpec(memory_space=pltpu.SMEM)]
        + [whole] * (5 + shards)
        + [anywhere] * len(grads),
        out_specs=[anywhere] * 3 + [whole],
        scratch_shapes=[pltpu.VMEM((length, heads * HEAD), jnp.bfloat16)] * 3
        + [pltpu.VMEM((length, length), jnp.bfloat16)] * 2
        + [pltpu.SemaphoreType.DMA((3 * heads,))],
        input_output_aliases={6 + shards + i: i for i in range(len(grads))},
        cost_estimate=pl.CostEstimate(
            flops=heads * 12 * length * length * HEAD,
            bytes_accessed=heads * 8 * length * HEAD * 2,
            transcendentals=heads * length * length,
        ),
        name="attend",
    )(where, *facts, gains, prior, *[in_vmem(b) for b in blocks], *grads)
    return out[:3], out[3]


def gathered_sum(spread, axes):
    return jnp.sum(lax.all_to_all(spread, axes, 0, 0, tiled=True), axis=0)


def body(
    query_in,
    key_in,
    value_in,
    latent_now,
    latent_next,
    norm_gains,
    rewards,
    step_index,
    token_count,
):
    segments = lax.axis_size("segment")
    replicas = lax.axis_size("dp")
    shards = lax.axis_size("seq")
    replica = lax.axis_index("dp")
    source = (lax.axis_index("segment") + segments - 1) % segments * replicas + replica
    where = jnp.stack([lax.axis_index("seq"), replica, source]).astype(jnp.int32)
    heads_local = query_in.shape[2] // HEAD // shards
    chunks = chunks_of(heads_local)

    plan = [(STAY, 0, heads_local)]
    for first, heads in chunks:
        plan += [(steps, first, heads) for steps in (SAME, FAR, BACK)]
    sent = pack(plan, shards, (query_in, key_in, value_in, latent_now, latent_next))
    arrived = {(steps, first): moved(a, steps) for (steps, first, _), a in zip(plan, sent)}

    facts = tuple(a[None] for a in (rewards, step_index, token_count))
    grads, partial = (), jnp.zeros((1, 2, HEAD), jnp.float32)
    places = (STAY, SAME, FAR, BACK)
    for c, (first, heads) in enumerate(chunks):
        blocks = [arrived[STAY, 0]] + [arrived[steps, first] for steps in places[1:]]
        copies = replicas if c == len(chunks) - 1 else 1
        grads, partial = attend(
            first, heads, heads_local, copies, places, where, facts, norm_gains, partial, blocks, grads
        )
    by_dp = gathered_sum(partial, "dp")
    others = segments * shards
    total = gathered_sum(jnp.broadcast_to(by_dp[None], (others, 2, HEAD)), ("segment", "seq"))
    return (*grads, total / (segments * replicas))


def solution(mesh):
    rows = P(("segment", "dp"), "seq", None)
    return jax.shard_map(
        body,
        mesh=mesh,
        in_specs=(rows,) * 5 + (P(),) * 4,
        out_specs=(P(("segment", "dp"), None, "seq"),) * 3 + (P(),),
        check_vma=False,
    )
```

```python
import functools
import math

import jax
import jax.numpy as jnp
from jax import lax
from jax.experimental import pallas as pl
from jax.experimental.pallas import tpu as pltpu
from jax.sharding import PartitionSpec as P

HEAD = 128
STEPS = 16
GROUP = 16
STAY, SAME, FAR, BACK = (0, 0), (-1, 1), (2, 2), (1, -1)


def chunks_of(heads):
    return ((0, heads - 1), (heads - 1, 1)) if heads > 1 else ((0, 1),)


def step_at(steps, replica, shards):
    return jnp.where(replica % 2 == 0, steps[0] % shards, steps[1] % shards)


def moved(value, steps):
    segments, replicas, shards = (lax.axis_size(a) for a in ("segment", "dp", "seq"))
    pairs = []
    for s in range(segments):
        for r in range(replicas):
            for q in range(shards):
                to = (q + steps[r % 2]) % shards
                pairs.append(
                    ((s * replicas + r) * shards + q, ((s + 1) % segments * replicas + r) * shards + to)
                )
    return lax.ppermute(value, ("segment", "dp", "seq"), pairs)


def pack_kernel(plan, shards, query, key, value, now, following, *rest):
    outs, (now_ref, next_ref, sems) = rest[: len(plan)], rest[len(plan) :]
    mine, replica = lax.axis_index("seq"), lax.axis_index("dp")
    width = query.shape[2] // shards
    late = [
        pltpu.make_async_copy(now.at[0], now_ref, sems.at[0]),
        pltpu.make_async_copy(following.at[0], next_ref, sems.at[1]),
    ]
    for copy in late:
        copy.start()
    places, copies = [], []
    for n, ((steps, first, heads), out) in enumerate(zip(plan, outs)):
        place = lax.rem(mine + step_at(steps, replica, shards), shards) * width + first * HEAD
        cols = pl.ds(pl.multiple_of(place, HEAD), heads * HEAD)
        places.append(cols)
        for at, array in enumerate((query, key, value)):
            copy = pltpu.make_async_copy(array.at[0, :, cols], out.at[at], sems.at[2 + 3 * n + at])
            copy.start()
            copies.append(copy)
    for copy in late:
        copy.wait()
    for cols, out in zip(places, outs):
        out[3] = (
            next_ref[:, cols].astype(jnp.float32) - now_ref[:, cols].astype(jnp.float32)
        ).astype(jnp.bfloat16)
    for copy in copies:
        copy.wait()


def pack(plan, shards, arrays):
    _, rows, width = arrays[0].shape
    return pl.pallas_call(
        functools.partial(pack_kernel, plan, shards),
        out_shape=[pltpu.VMEM((4, rows, heads * HEAD), jnp.bfloat16) for _, _, heads in plan],
        in_specs=[pl.BlockSpec(memory_space=pl.ANY)] * 5,
        out_specs=[pl.BlockSpec(memory_space=pltpu.VMEM)] * len(plan),
        scratch_shapes=[pltpu.VMEM((rows, width), jnp.bfloat16)] * 2
        + [pltpu.SemaphoreType.DMA((2 + 3 * len(plan),))],
        cost_estimate=pl.CostEstimate(flops=1, bytes_accessed=2 << 20, transcendentals=0),
        name="pack",
    )(*arrays)


def slot_scalars(source, rewards, steps, counts):
    total = rewards.shape[1]
    lane = lax.broadcasted_iota(jnp.int32, (1, total), 1)
    of_group = (lane // GROUP) == (source // GROUP)
    of_slot = lane == source

    def picked(which, row):
        return jnp.sum(jnp.where(which, row, jnp.zeros_like(row)), axis=1, keepdims=True)

    mean = picked(of_group, rewards) / GROUP
    spread = jnp.sqrt(picked(of_group, (rewards - mean) ** 2) / GROUP)
    advantage = (picked(of_slot, rewards) - mean) / jnp.maximum(spread, jnp.float32(0.25))
    index = picked(of_slot, steps.astype(jnp.float32))

    def sigma(k):
        level = 1.0 - k / STEPS
        return 7.0 * level / (1.0 + 6.0 * level)

    delta = sigma(index) - sigma(index + 1.0)
    count = picked(of_slot, counts.astype(jnp.float32))
    return advantage, delta, count


def dot(a, b, dims):
    return lax.dot_general(a, b, (dims, ((), ())), preferred_element_type=jnp.float32)


def attend_kernel(first, places, has_prior, rewards, steps, counts, gains, *rest):
    blocks, rest = rest[: len(places)], rest[len(places) :]
    prior = rest[0] if has_prior else None
    dq_hbm, dk_hbm, dv_hbm, dg_ref, dq_ref, dk_ref, dv_ref, e_ref, ds_ref, sems = rest[-10:]
    mine, replica = lax.axis_index("seq"), lax.axis_index("dp")
    segments, replicas = lax.axis_size("segment"), lax.axis_size("dp")
    source = lax.rem(lax.axis_index("segment") + segments - 1, segments) * replicas + replica
    advantage, delta, count = slot_scalars(source, rewards[...], steps[...], counts[...])
    shards, rows = len(blocks), blocks[0].shape[1]
    heads = dq_ref.shape[1] // HEAD
    each = [(h, d) for h in range(heads) for d in range(shards)]
    gain_q, gain_k = gains[0:1, :], gains[1:2, :]
    inv_root = 1.0 / math.sqrt(HEAD)
    log2e = math.log2(math.e)
    starts, alive = [], []
    for place in places:
        start = lax.rem(mine - step_at(place, replica, shards) + shards, shards) * rows
        starts.append(pl.multiple_of(start, rows))
        token = lax.broadcasted_iota(jnp.int32, (rows, HEAD), 0) + start
        alive.append(jnp.where(token.astype(jnp.float32) < count, jnp.float32(1.0), 0.0))
    alive_low = [a.astype(jnp.bfloat16) for a in alive]
    keep = jnp.concatenate(alive_low, axis=0)

    def part(h, d, at):
        block = blocks[d]
        skip = first * HEAD if block.shape[2] > dq_ref.shape[1] else 0
        return block[at, :, skip + h * HEAD : skip + (h + 1) * HEAD]

    def normed(h, d, at):
        wide = part(h, d, at).astype(jnp.float32)
        scale = lax.rsqrt(jnp.mean(wide * wide, axis=-1, keepdims=True) + 1e-06)
        if at == 1:
            scale = scale * alive[d]
        return wide * scale, scale

    def stack(piece, h):
        return jnp.concatenate([piece[h, d] for d in range(shards)], axis=0)

    def cols(h):
        return slice(h * HEAD, (h + 1) * HEAD)

    copies = []

    def give(kind, staged, hbm, h):
        copy = pltpu.make_async_copy(
            staged.at[:, cols(h)],
            hbm.at[0, :, pl.ds((first + h) * HEAD, HEAD)],
            sems.at[3 * h + kind],
        )
        copy.start()
        copies.append(copy)

    q_hat, q_scale, q_rows, k_hat, k_scale, k_rows, v_rows = ({} for _ in range(7))
    for h, d in each:
        k_hat[h, d], k_scale[h, d] = normed(h, d, 1)
        k_rows[h, d] = (k_hat[h, d] * gain_k).astype(jnp.bfloat16)
    for h, d in each:
        q_hat[h, d], q_scale[h, d] = normed(h, d, 0)
        q_rows[h, d] = (q_hat[h, d] * (gain_q * (inv_root * log2e))).astype(jnp.bfloat16)
        v_rows[h, d] = part(h, d, 2) * alive_low[d]
    keys = [stack(k_rows, h) for h in range(heads)]
    values = [stack(v_rows, h) for h in range(heads)]

    e = {}
    for h, d in each:
        e[h, d] = jnp.exp2(dot(q_rows[h, d], keys[h], ((1,), (1,)))).astype(jnp.bfloat16)
        e_ref[h, d * rows : (d + 1) * rows, :] = e[h, d]
    pull, level = {}, {}
    for h, d in each:
        both = dot(e[h, d], jnp.concatenate([values[h], keep], axis=1), ((1,), (0,)))
        share = 1.0 / both[:, HEAD:]
        velocity = both[:, :HEAD] * share
        change = part(h, d, 3).astype(jnp.float32) + delta * velocity
        pull[h, d] = (change * (share * (alive[d] * advantage))).astype(jnp.bfloat16)
        level[h, d] = jnp.sum(
            pull[h, d].astype(jnp.float32) * velocity, axis=-1, keepdims=True
        )
    ds = {}
    for h, d in each:
        d_weights = dot(pull[h, d], values[h], ((1,), (1,)))
        ds[h, d] = e_ref[h, d * rows : (d + 1) * rows, :] * (d_weights - level[h, d]).astype(
            jnp.bfloat16
        )
        ds_ref[h, d * rows : (d + 1) * rows, :] = ds[h, d]
    d_values = [dot(e_ref[h], stack(pull, h), ((0,), (0,))) for h in range(heads)]
    d_queries = {}
    for h, d in each:
        d_queries[h, d] = dot(ds[h, d], keys[h], ((1,), (0,)))
    d_keys = [dot(ds_ref[h], stack(q_rows, h), ((0,), (0,))) for h in range(heads)]

    def unnormed(d_rows, hat, scale, gain):
        shared = d_rows * hat
        inner = d_rows * gain - hat * jnp.mean(shared * gain, axis=-1, keepdims=True)
        return (inner * scale).astype(jnp.bfloat16), jnp.sum(shared, axis=0, keepdims=True)

    for h in range(heads):
        for d in range(shards):
            d_rows = d_values[h][d * rows : (d + 1) * rows].astype(jnp.bfloat16) * alive_low[d]
            dv_ref[pl.ds(starts[d], rows), cols(h)] = d_rows
        give(2, dv_ref, dv_hbm, h)
    grad_gq = jnp.zeros((1, HEAD), jnp.float32)
    for h in range(heads):
        for d in range(shards):
            out, summed = unnormed(d_queries[h, d], q_hat[h, d], q_scale[h, d], gain_q * inv_root)
            dq_ref[pl.ds(starts[d], rows), cols(h)] = out
            grad_gq += summed
        give(0, dq_ref, dq_hbm, h)
    grad_gk = jnp.zeros((1, HEAD), jnp.float32)
    for h in range(heads):
        for d in range(shards):
            d_rows = d_keys[h][d * rows : (d + 1) * rows]
            out, summed = unnormed(d_rows, k_hat[h, d], k_scale[h, d], gain_k * (1.0 / log2e))
            dk_ref[pl.ds(starts[d], rows), cols(h)] = out
            grad_gk += summed
        give(1, dk_ref, dk_hbm, h)
    total = jnp.concatenate([grad_gq * inv_root, grad_gk * (1.0 / log2e)], axis=0)[None]
    if has_prior:
        total = total + prior[0:1]
    dg_ref[...] = jnp.broadcast_to(total, dg_ref.shape)
    for copy in copies:
        copy.wait()


def in_vmem(array):
    return pltpu.with_memory_space_constraint(array, pltpu.VMEM)


def attend(first, heads, heads_local, copies, places, facts, gains, blocks, prior, grads):
    shards = len(blocks)
    length = blocks[0].shape[1] * shards
    whole, anywhere = pl.BlockSpec(memory_space=pltpu.VMEM), pl.BlockSpec(memory_space=pl.ANY)
    grad_shape = jax.ShapeDtypeStruct((1, length, heads_local * HEAD), jnp.bfloat16)
    inputs = [*facts, gains, *[in_vmem(b) for b in blocks]] + ([] if prior is None else [prior])
    out = pl.pallas_call(
        functools.partial(attend_kernel, first, places, prior is not None),
        out_shape=[grad_shape] * 3 + [jax.ShapeDtypeStruct((copies, 2, HEAD), jnp.float32)],
        in_specs=[whole] * len(inputs) + [anywhere] * len(grads),
        out_specs=[anywhere] * 3 + [whole],
        scratch_shapes=[pltpu.VMEM((length, heads * HEAD), jnp.bfloat16)] * 3
        + [pltpu.VMEM((heads, length, length), jnp.bfloat16)] * 2
        + [pltpu.SemaphoreType.DMA((3 * heads,))],
        input_output_aliases={len(inputs) + i: i for i in range(len(grads))},
        cost_estimate=pl.CostEstimate(
            flops=heads * 12 * length * length * HEAD,
            bytes_accessed=heads * 8 * length * HEAD * 2,
            transcendentals=heads * length * length,
        ),
        name="attend",
    )(*inputs, *grads)
    return out[:3], out[3]


def gathered_sum(spread, axes):
    return jnp.sum(lax.all_to_all(spread, axes, 0, 0, tiled=True), axis=0)


def body(
    query_in,
    key_in,
    value_in,
    latent_now,
    latent_next,
    norm_gains,
    rewards,
    step_index,
    token_count,
):
    segments = lax.axis_size("segment")
    replicas = lax.axis_size("dp")
    shards = lax.axis_size("seq")
    heads_local = query_in.shape[2] // HEAD // shards
    chunks = chunks_of(heads_local)

    plan = [(STAY, 0, heads_local)]
    for first, heads in chunks:
        plan += [(steps, first, heads) for steps in (SAME, FAR, BACK)]
    sent = pack(plan, shards, (query_in, key_in, value_in, latent_now, latent_next))
    arrived = {(steps, first): moved(a, steps) for (steps, first, _), a in zip(plan, sent)}

    facts = tuple(a[None] for a in (rewards, step_index, token_count))
    grads, partial = (), None
    places = (STAY, SAME, FAR, BACK)
    for c, (first, heads) in enumerate(chunks):
        blocks = [arrived[STAY, 0]] + [arrived[steps, first] for steps in places[1:]]
        copies = replicas if c == len(chunks) - 1 else 1
        grads, partial = attend(
            first, heads, heads_local, copies, places, facts, norm_gains, blocks, partial, grads
        )
    by_dp = gathered_sum(partial, "dp")
    others = segments * shards
    total = gathered_sum(jnp.broadcast_to(by_dp[None], (others, 2, HEAD)), ("segment", "seq"))
    return (*grads, total / (segments * replicas))


def solution(mesh):
    rows = P(("segment", "dp"), "seq", None)
    return jax.shard_map(
        body,
        mesh=mesh,
        in_specs=(rows,) * 5 + (P(),) * 4,
        out_specs=(P(("segment", "dp"), None, "seq"),) * 3 + (P(),),
        check_vma=False,
    )
```

```python
import functools
import math

import jax
import jax.numpy as jnp
from jax import lax
from jax.experimental import pallas as pl
from jax.experimental.pallas import tpu as pltpu
from jax.sharding import PartitionSpec as P


HEAD = 128
STEPS = 16
GROUP = 16
STAY, SAME, FAR, BACK = (0, 0), (-1, 1), (2, 2), (1, -1)
PLACES = (SAME, FAR, BACK, STAY)
QUERY, KEY, VALUE, CHANGE = range(4)


def payloads(heads):
    last = heads - 1
    early = ((QUERY, 0, heads), (KEY, 0, heads), (VALUE, 0, last), (CHANGE, 0, last))
    late = ((VALUE, last, 1), (CHANGE, last, 1))
    return early, late, tuple((array, 0, heads) for array in range(4))


def lanes_of(message):
    return sum(heads for _, _, heads in message) * HEAD


def find(message, array, head):
    at = 0
    for kind, first, heads in message:
        if kind == array and first <= head < first + heads:
            return at + (head - first) * HEAD
        at += heads * HEAD
    return None


def step_at(steps, replica, shards):
    return jnp.where(replica % 2 == 0, steps[0] % shards, steps[1] % shards)


def moved(value, steps):
    segments, replicas, shards = (lax.axis_size(a) for a in ("segment", "dp", "seq"))
    pairs = []
    for s in range(segments):
        for r in range(replicas):
            for q in range(shards):
                to = (q + steps[r % 2]) % shards
                pairs.append(
                    ((s * replicas + r) * shards + q, ((s + 1) % segments * replicas + r) * shards + to)
                )
    return lax.ppermute(value, ("segment", "dp", "seq"), pairs)


def pack_kernel(plan, shards, query, key, value, now, following, *rest):
    outs, (now_ref, next_ref, sems) = rest[: len(plan)], rest[len(plan) :]
    mine, replica = lax.axis_index("seq"), lax.axis_index("dp")
    width = query.shape[2] // shards
    late = [
        pltpu.make_async_copy(now.at[0], now_ref, sems.at[0]),
        pltpu.make_async_copy(following.at[0], next_ref, sems.at[1]),
    ]
    for copy in late:
        copy.start()
    copies, changes = [], []
    for (steps, message), out in zip(plan, outs):
        base = lax.rem(mine + step_at(steps, replica, shards), shards) * width
        at = 0
        for array, first, heads in message:
            size = heads * HEAD
            source = pl.ds(pl.multiple_of(base + first * HEAD, HEAD), size)
            if array == CHANGE:
                changes.append((source, out, slice(at, at + size)))
            else:
                copy = pltpu.make_async_copy(
                    (query, key, value)[array].at[0, :, source],
                    out.at[:, at : at + size],
                    sems.at[2 + len(copies)],
                )
                copy.start()
                copies.append(copy)
            at += size
    for copy in late:
        copy.wait()
    for source, out, lanes in changes:
        out[:, lanes] = (
            next_ref[:, source].astype(jnp.float32) - now_ref[:, source].astype(jnp.float32)
        ).astype(jnp.bfloat16)
    for copy in copies:
        copy.wait()


def pack(plan, shards, arrays):
    _, rows, width = arrays[0].shape
    return pl.pallas_call(
        functools.partial(pack_kernel, plan, shards),
        out_shape=[pltpu.VMEM((rows, lanes_of(message)), jnp.bfloat16) for _, message in plan],
        in_specs=[pl.BlockSpec(memory_space=pl.ANY)] * 5,
        out_specs=[pl.BlockSpec(memory_space=pltpu.VMEM)] * len(plan),
        scratch_shapes=[pltpu.VMEM((rows, width), jnp.bfloat16)] * 2
        + [pltpu.SemaphoreType.DMA((2 + 3 * len(plan),))],
        cost_estimate=pl.CostEstimate(flops=1, bytes_accessed=2 << 20, transcendentals=0),
        name="pack",
    )(*arrays)


def slot_scalars(source, rewards, steps, counts):
    total = rewards.shape[1]
    lane = lax.broadcasted_iota(jnp.int32, (1, total), 1)
    of_group = (lane // GROUP) == (source // GROUP)
    of_slot = lane == source

    def picked(which, row):
        return jnp.sum(jnp.where(which, row, jnp.zeros_like(row)), axis=1, keepdims=True)

    mean = picked(of_group, rewards) / GROUP
    spread = jnp.sqrt(picked(of_group, (rewards - mean) ** 2) / GROUP)
    advantage = (picked(of_slot, rewards) - mean) / jnp.maximum(spread, jnp.float32(0.25))
    index = picked(of_slot, steps.astype(jnp.float32))

    def sigma(k):
        level = 1.0 - k / STEPS
        return 7.0 * level / (1.0 + 6.0 * level)

    delta = sigma(index) - sigma(index + 1.0)
    count = picked(of_slot, counts.astype(jnp.float32))
    return advantage, delta, count


def dot(a, b, dims):
    return lax.dot_general(a, b, (dims, ((), ())), preferred_element_type=jnp.float32)


def attend_kernel(messages, first, heads, ahead, given, rewards, steps, counts, gains, *rest):
    shards = len(messages)
    texts = [[(text, rest[at]) for text, at in place] for place in messages]
    rest = rest[sum(len(place) for place in messages) :]
    e_given, prior = (rest[0], rest[1]) if given else (None, None)
    if ahead:
        e_next, rest = rest[-7], rest[:-7] + rest[-6:]
    dq_hbm, dk_hbm, dv_hbm, dg_ref, dq_ref, dk_ref, dv_ref, e_ref, ds_ref, sems = rest[-10:]
    mine, replica = lax.axis_index("seq"), lax.axis_index("dp")
    segments, replicas = lax.axis_size("segment"), lax.axis_size("dp")
    source = lax.rem(lax.axis_index("segment") + segments - 1, segments) * replicas + replica
    advantage, delta, count = slot_scalars(source, rewards[...], steps[...], counts[...])
    rows = texts[0][0][1].shape[0]
    each = [(h, d) for h in range(heads) for d in range(shards)]
    scored = [(h, d) for h in range(heads + ahead) for d in range(shards)]
    gain_q, gain_k = gains[0:1, :], gains[1:2, :]
    inv_root = 1.0 / math.sqrt(HEAD)
    log2e = math.log2(math.e)
    starts, alive = [], []
    for place in PLACES:
        start = lax.rem(mine - step_at(place, replica, shards) + shards, shards) * rows
        starts.append(pl.multiple_of(start, rows))
        token = lax.broadcasted_iota(jnp.int32, (rows, HEAD), 0) + start
        alive.append(jnp.where(token.astype(jnp.float32) < count, jnp.float32(1.0), 0.0))
    alive_low = [a.astype(jnp.bfloat16) for a in alive]
    keep = jnp.concatenate(alive_low, axis=0)

    def part(h, d, at):
        for message, text in texts[d]:
            lane = find(message, at, first + h)
            if lane is not None:
                return text[:, lane : lane + HEAD]
        raise ValueError((h, at))

    def normed(h, d, at):
        wide = part(h, d, at).astype(jnp.float32)
        scale = lax.rsqrt(jnp.mean(wide * wide, axis=-1, keepdims=True) + 1e-06)
        if at == KEY:
            scale = scale * alive[d]
        return wide * scale, scale

    def stack(piece, h):
        return jnp.concatenate([piece[h, d] for d in range(shards)], axis=0)

    def cols(h):
        return slice(h * HEAD, (h + 1) * HEAD)

    copies = []

    def give(kind, staged, hbm, h):
        copy = pltpu.make_async_copy(
            staged.at[:, cols(h)],
            hbm.at[0, :, pl.ds((first + h) * HEAD, HEAD)],
            sems.at[3 * h + kind],
        )
        copy.start()
        copies.append(copy)

    q_hat, q_scale, q_rows, k_hat, k_scale, k_rows, v_rows = ({} for _ in range(7))
    for h, d in scored:
        k_hat[h, d], k_scale[h, d] = normed(h, d, KEY)
        k_rows[h, d] = (k_hat[h, d] * gain_k).astype(jnp.bfloat16)
    for h, d in scored:
        q_hat[h, d], q_scale[h, d] = normed(h, d, QUERY)
        q_rows[h, d] = (q_hat[h, d] * (gain_q * (inv_root * log2e))).astype(jnp.bfloat16)
    for h, d in each:
        v_rows[h, d] = part(h, d, VALUE) * alive_low[d]
    keys = [stack(k_rows, h) for h in range(heads + ahead)]
    values = [stack(v_rows, h) for h in range(heads)]

    e = {}
    weights = [e_given if given else e_ref.at[h] for h in range(heads)]

    def of(d):
        return slice(d * rows, (d + 1) * rows)

    def weigh(h, d, to):
        e[h, d] = jnp.exp2(dot(q_rows[h, d], keys[h], ((1,), (1,)))).astype(jnp.bfloat16)
        to[of(d), :] = e[h, d]

    for h, d in each:
        if given:
            e[h, d] = e_given[of(d), :]
        else:
            weigh(h, d, weights[h])
    pull, level = {}, {}
    for h, d in each:
        both = dot(e[h, d], jnp.concatenate([values[h], keep], axis=1), ((1,), (0,)))
        share = 1.0 / both[:, HEAD:]
        velocity = both[:, :HEAD] * share
        change = part(h, d, CHANGE).astype(jnp.float32) + delta * velocity
        pull[h, d] = (change * (share * (alive[d] * advantage))).astype(jnp.bfloat16)
        level[h, d] = jnp.sum(
            pull[h, d].astype(jnp.float32) * velocity, axis=-1, keepdims=True
        )
    ds = {}
    for h, d in each:
        d_weights = dot(pull[h, d], values[h], ((1,), (1,)))
        ds[h, d] = weights[h][of(d), :] * (d_weights - level[h, d]).astype(
            jnp.bfloat16
        )
        ds_ref[h, d * rows : (d + 1) * rows, :] = ds[h, d]
    if ahead:
        for d in range(shards):
            weigh(heads, d, e_next)
    d_values = [dot(weights[h][...], stack(pull, h), ((0,), (0,))) for h in range(heads)]
    d_queries = {}
    for h, d in each:
        d_queries[h, d] = dot(ds[h, d], keys[h], ((1,), (0,)))
    d_keys = [dot(ds_ref[h], stack(q_rows, h), ((0,), (0,))) for h in range(heads)]

    def unnormed(d_rows, hat, scale, gain):
        shared = d_rows * hat
        inner = d_rows * gain - hat * jnp.mean(shared * gain, axis=-1, keepdims=True)
        return (inner * scale).astype(jnp.bfloat16), jnp.sum(shared, axis=0, keepdims=True)

    for h in range(heads):
        for d in range(shards):
            d_rows = d_values[h][d * rows : (d + 1) * rows].astype(jnp.bfloat16) * alive_low[d]
            dv_ref[pl.ds(starts[d], rows), cols(h)] = d_rows
        give(2, dv_ref, dv_hbm, h)
    grad_gq = jnp.zeros((1, HEAD), jnp.float32)
    for h in range(heads):
        for d in range(shards):
            out, summed = unnormed(d_queries[h, d], q_hat[h, d], q_scale[h, d], gain_q * inv_root)
            dq_ref[pl.ds(starts[d], rows), cols(h)] = out
            grad_gq += summed
        give(0, dq_ref, dq_hbm, h)
    grad_gk = jnp.zeros((1, HEAD), jnp.float32)
    for h in range(heads):
        for d in range(shards):
            d_rows = d_keys[h][d * rows : (d + 1) * rows]
            out, summed = unnormed(d_rows, k_hat[h, d], k_scale[h, d], gain_k * (1.0 / log2e))
            dk_ref[pl.ds(starts[d], rows), cols(h)] = out
            grad_gk += summed
        give(1, dk_ref, dk_hbm, h)
    total = jnp.concatenate([grad_gq * inv_root, grad_gk * (1.0 / log2e)], axis=0)[None]
    if prior is not None:
        total = total + prior[0:1]
    dg_ref[...] = jnp.broadcast_to(total, dg_ref.shape)
    for copy in copies:
        copy.wait()


def in_vmem(array):
    return pltpu.with_memory_space_constraint(array, pltpu.VMEM)


def attend(messages, texts, first, heads, ahead, heads_local, copies, facts, gains, carried, grads):
    shards, rows = len(messages), texts[0].shape[0]
    length = rows * shards
    whole, anywhere = pl.BlockSpec(memory_space=pltpu.VMEM), pl.BlockSpec(memory_space=pl.ANY)
    inputs = [*facts, gains, *[in_vmem(t) for t in texts]]
    if carried:
        inputs += [in_vmem(carried[0]), carried[1]]
    grad_shape = jax.ShapeDtypeStruct((1, length, heads_local * HEAD), jnp.bfloat16)
    return pl.pallas_call(
        functools.partial(attend_kernel, messages, first, heads, ahead, bool(carried)),
        out_shape=[grad_shape] * 3
        + [jax.ShapeDtypeStruct((copies, 2, HEAD), jnp.float32)]
        + [pltpu.VMEM((length, length), jnp.bfloat16)] * ahead,
        in_specs=[whole] * len(inputs) + [anywhere] * len(grads),
        out_specs=[anywhere] * 3 + [whole] * (1 + ahead),
        scratch_shapes=[pltpu.VMEM((length, heads * HEAD), jnp.bfloat16)] * 3
        + [pltpu.VMEM((heads, length, length), jnp.bfloat16)] * 2
        + [pltpu.SemaphoreType.DMA((3 * heads,))],
        input_output_aliases={len(inputs) + i: i for i in range(len(grads))},
        cost_estimate=pl.CostEstimate(
            flops=heads * 12 * length * length * HEAD,
            bytes_accessed=heads * 8 * length * HEAD * 2,
            transcendentals=heads * length * length,
        ),
        name="attend",
    )(*inputs, *grads)


def gathered_sum(spread, axes):
    return jnp.sum(lax.all_to_all(spread, axes, 0, 0, tiled=True), axis=0)


def body(
    query_in,
    key_in,
    value_in,
    latent_now,
    latent_next,
    norm_gains,
    rewards,
    step_index,
    token_count,
):
    segments = lax.axis_size("segment")
    replicas = lax.axis_size("dp")
    shards = lax.axis_size("seq")
    heads = query_in.shape[2] // HEAD // shards
    early, late, both = payloads(heads)

    plan = [(steps, early) for steps in PLACES if steps != STAY]
    plan += [(STAY, both)]
    plan += [(steps, late) for steps in PLACES if steps != STAY]
    sent = pack(plan, shards, (query_in, key_in, value_in, latent_now, latent_next))
    arrived = {}
    for entry, a in zip(plan, sent):
        arrived[entry] = moved(a, entry[0])

    facts = tuple(a[None] for a in (rewards, step_index, token_count))
    first_texts = [arrived[steps, both if steps == STAY else early] for steps in PLACES]
    later_texts = [arrived[steps, late] for steps in PLACES if steps != STAY]
    first_messages = tuple(
        ((both if steps == STAY else early, n),) for n, steps in enumerate(PLACES)
    )
    last_messages = tuple(
        entry if steps == STAY else (*entry, (late, shards + n))
        for n, (steps, entry) in enumerate(zip(PLACES, first_messages))
    )
    out = attend(
        first_messages, first_texts, 0, heads - 1, 1, heads, 1, facts, norm_gains, (), ()
    )
    grads, carried = out[:3], (out[4], out[3])
    out = attend(
        last_messages,
        first_texts + later_texts,
        heads - 1,
        1,
        0,
        heads,
        replicas,
        facts,
        norm_gains,
        carried,
        grads,
    )
    grads, partial = out[:3], out[3]
    by_dp = gathered_sum(partial, "dp")
    others = segments * shards
    total = gathered_sum(jnp.broadcast_to(by_dp[None], (others, 2, HEAD)), ("segment", "seq"))
    return (*grads, total / (segments * replicas))


def solution(mesh):
    rows = P(("segment", "dp"), "seq", None)
    return jax.shard_map(
        body,
        mesh=mesh,
        in_specs=(rows,) * 5 + (P(),) * 4,
        out_specs=(P(("segment", "dp"), None, "seq"),) * 3 + (P(),),
        check_vma=False,
    )
```

```python
import functools
import math

import jax
import jax.numpy as jnp
from jax import lax
from jax.experimental import pallas as pl
from jax.experimental.pallas import tpu as pltpu
from jax.sharding import PartitionSpec as P

HEAD = 128
STEPS = 16
GROUP = 16
STAY, SAME, FAR, BACK = (0, 0), (-1, 1), (2, 2), (1, -1)


def chunks_of(heads):
    return ((0, heads - 1), (heads - 1, 1)) if heads > 1 else ((0, 1),)


def step_at(steps, replica, shards):
    return jnp.where(replica % 2 == 0, steps[0] % shards, steps[1] % shards)


def moved(value, steps):
    segments, replicas, shards = (lax.axis_size(a) for a in ("segment", "dp", "seq"))
    pairs = []
    for s in range(segments):
        for r in range(replicas):
            for q in range(shards):
                to = (q + steps[r % 2]) % shards
                pairs.append(
                    ((s * replicas + r) * shards + q, ((s + 1) % segments * replicas + r) * shards + to)
                )
    return lax.ppermute(value, ("segment", "dp", "seq"), pairs)


def pack_kernel(plan, shards, query, key, value, now, following, *rest):
    outs, (now_ref, next_ref, sems) = rest[: len(plan)], rest[len(plan) :]
    mine, replica = lax.axis_index("seq"), lax.axis_index("dp")
    width = query.shape[2] // shards
    late = [
        pltpu.make_async_copy(now.at[0], now_ref, sems.at[0]),
        pltpu.make_async_copy(following.at[0], next_ref, sems.at[1]),
    ]
    for copy in late:
        copy.start()
    places, copies = [], []
    for n, ((steps, first, heads), out) in enumerate(zip(plan, outs)):
        place = lax.rem(mine + step_at(steps, replica, shards), shards) * width + first * HEAD
        cols = pl.ds(pl.multiple_of(place, HEAD), heads * HEAD)
        places.append(cols)
        for at, array in enumerate((query, key, value)):
            copy = pltpu.make_async_copy(array.at[0, :, cols], out.at[at], sems.at[2 + 3 * n + at])
            copy.start()
            copies.append(copy)
    for copy in late:
        copy.wait()
    for cols, out in zip(places, outs):
        out[3] = (
            next_ref[:, cols].astype(jnp.float32) - now_ref[:, cols].astype(jnp.float32)
        ).astype(jnp.bfloat16)
    for copy in copies:
        copy.wait()


def pack(plan, shards, arrays):
    _, rows, width = arrays[0].shape
    return pl.pallas_call(
        functools.partial(pack_kernel, plan, shards),
        out_shape=[pltpu.VMEM((4, rows, heads * HEAD), jnp.bfloat16) for _, _, heads in plan],
        in_specs=[pl.BlockSpec(memory_space=pl.ANY)] * 5,
        out_specs=[pl.BlockSpec(memory_space=pltpu.VMEM)] * len(plan),
        scratch_shapes=[pltpu.VMEM((rows, width), jnp.bfloat16)] * 2
        + [pltpu.SemaphoreType.DMA((2 + 3 * len(plan),))],
        cost_estimate=pl.CostEstimate(flops=1, bytes_accessed=2 << 20, transcendentals=0),
        name="pack",
    )(*arrays)


def slot_scalars(source, rewards, steps, counts):
    total = rewards.shape[1]
    lane = lax.broadcasted_iota(jnp.int32, (1, total), 1)
    of_group = (lane // GROUP) == (source // GROUP)
    of_slot = lane == source

    def picked(which, row):
        return jnp.sum(jnp.where(which, row, jnp.zeros_like(row)), axis=1, keepdims=True)

    mean = picked(of_group, rewards) / GROUP
    spread = jnp.sqrt(picked(of_group, (rewards - mean) ** 2) / GROUP)
    advantage = (picked(of_slot, rewards) - mean) / jnp.maximum(spread, jnp.float32(0.25))
    index = picked(of_slot, steps.astype(jnp.float32))

    def sigma(k):
        level = 1.0 - k / STEPS
        return 7.0 * level / (1.0 + 6.0 * level)

    delta = sigma(index) - sigma(index + 1.0)
    count = picked(of_slot, counts.astype(jnp.float32))
    return advantage, delta, count


def dot(a, b, dims):
    return lax.dot_general(a, b, (dims, ((), ())), preferred_element_type=jnp.float32)


def attend_kernel(first, places, has_prior, rewards, steps, counts, gains, *rest):
    blocks, rest = rest[: len(places)], rest[len(places) :]
    prior = rest[0] if has_prior else None
    dq_hbm, dk_hbm, dv_hbm, dg_ref, dq_ref, dk_ref, dv_ref, e_ref, ds_ref, sems = rest[-10:]
    mine, replica = lax.axis_index("seq"), lax.axis_index("dp")
    segments, replicas = lax.axis_size("segment"), lax.axis_size("dp")
    source = lax.rem(lax.axis_index("segment") + segments - 1, segments) * replicas + replica
    advantage, delta, count = slot_scalars(source, rewards[...], steps[...], counts[...])
    shards, rows = len(blocks), blocks[0].shape[1]
    heads = dq_ref.shape[1] // HEAD
    each = [(h, d) for h in range(heads) for d in range(shards)]
    gain_q, gain_k = gains[0:1, :], gains[1:2, :]
    inv_root = 1.0 / math.sqrt(HEAD)
    log2e = math.log2(math.e)
    starts, alive = [], []
    for place in places:
        start = lax.rem(mine - step_at(place, replica, shards) + shards, shards) * rows
        starts.append(pl.multiple_of(start, rows))
        token = lax.broadcasted_iota(jnp.int32, (rows, HEAD), 0) + start
        alive.append(jnp.where(token.astype(jnp.float32) < count, jnp.float32(1.0), 0.0))
    alive_low = [a.astype(jnp.bfloat16) for a in alive]
    keep = jnp.concatenate(alive_low, axis=0)

    def part(h, d, at):
        block = blocks[d]
        skip = first * HEAD if block.shape[2] > dq_ref.shape[1] else 0
        return block[at, :, skip + h * HEAD : skip + (h + 1) * HEAD]

    def normed(h, d, at):
        wide = part(h, d, at).astype(jnp.float32)
        scale = lax.rsqrt(jnp.mean(wide * wide, axis=-1, keepdims=True) + 1e-06)
        if at == 1:
            scale = scale * alive[d]
        return wide * scale, scale

    def stack(piece, h):
        return jnp.concatenate([piece[h, d] for d in range(shards)], axis=0)

    def cols(h):
        return slice(h * HEAD, (h + 1) * HEAD)

    copies = []

    def give(kind, staged, hbm, h):
        copy = pltpu.make_async_copy(
            staged.at[:, cols(h)],
            hbm.at[0, :, pl.ds((first + h) * HEAD, HEAD)],
            sems.at[3 * h + kind],
        )
        copy.start()
        copies.append(copy)

    q_hat, q_scale, q_rows, k_hat, k_scale, k_rows, v_rows = ({} for _ in range(7))
    for h, d in each:
        k_hat[h, d], k_scale[h, d] = normed(h, d, 1)
        k_rows[h, d] = (k_hat[h, d] * gain_k).astype(jnp.bfloat16)
    for h, d in each:
        q_hat[h, d], q_scale[h, d] = normed(h, d, 0)
        q_rows[h, d] = (q_hat[h, d] * (gain_q * (inv_root * log2e))).astype(jnp.bfloat16)
        v_rows[h, d] = part(h, d, 2) * alive_low[d]
    keys = [stack(k_rows, h) for h in range(heads)]
    values = [stack(v_rows, h) for h in range(heads)]

    e = {}
    for h, d in each:
        e[h, d] = jnp.exp2(dot(q_rows[h, d], keys[h], ((1,), (1,)))).astype(jnp.bfloat16)
        e_ref[h, d * rows : (d + 1) * rows, :] = e[h, d]
    pull, level = {}, {}
    for h, d in each:
        both = dot(e[h, d], jnp.concatenate([values[h], keep], axis=1), ((1,), (0,)))
        share = 1.0 / both[:, HEAD:]
        velocity = both[:, :HEAD] * share
        change = part(h, d, 3).astype(jnp.float32) + delta * velocity
        pull[h, d] = (change * (share * (alive[d] * advantage))).astype(jnp.bfloat16)
        level[h, d] = jnp.sum(
            pull[h, d].astype(jnp.float32) * velocity, axis=-1, keepdims=True
        )
    ds = {}
    for h, d in each:
        d_weights = dot(pull[h, d], values[h], ((1,), (1,)))
        ds[h, d] = e_ref[h, d * rows : (d + 1) * rows, :] * (d_weights - level[h, d]).astype(
            jnp.bfloat16
        )
        ds_ref[h, d * rows : (d + 1) * rows, :] = ds[h, d]
    d_values = [dot(e_ref[h], stack(pull, h), ((0,), (0,))) for h in range(heads)]
    d_queries = {}
    for h, d in each:
        d_queries[h, d] = dot(ds[h, d], keys[h], ((1,), (0,)))
    d_keys = [dot(ds_ref[h], stack(q_rows, h), ((0,), (0,))) for h in range(heads)]

    def unnormed(d_rows, hat, scale, gain):
        shared = d_rows * hat
        inner = d_rows * gain - hat * jnp.mean(shared * gain, axis=-1, keepdims=True)
        return (inner * scale).astype(jnp.bfloat16), jnp.sum(shared, axis=0, keepdims=True)

    for h in range(heads):
        for d in range(shards):
            d_rows = d_values[h][d * rows : (d + 1) * rows].astype(jnp.bfloat16) * alive_low[d]
            dv_ref[pl.ds(starts[d], rows), cols(h)] = d_rows
        give(2, dv_ref, dv_hbm, h)
    grad_gq = jnp.zeros((1, HEAD), jnp.float32)
    for h in range(heads):
        for d in range(shards):
            out, summed = unnormed(d_queries[h, d], q_hat[h, d], q_scale[h, d], gain_q * inv_root)
            dq_ref[pl.ds(starts[d], rows), cols(h)] = out
            grad_gq += summed
        give(0, dq_ref, dq_hbm, h)
    grad_gk = jnp.zeros((1, HEAD), jnp.float32)
    for h in range(heads):
        for d in range(shards):
            d_rows = d_keys[h][d * rows : (d + 1) * rows]
            out, summed = unnormed(d_rows, k_hat[h, d], k_scale[h, d], gain_k * (1.0 / log2e))
            dk_ref[pl.ds(starts[d], rows), cols(h)] = out
            grad_gk += summed
        give(1, dk_ref, dk_hbm, h)
    total = jnp.concatenate([grad_gq * inv_root, grad_gk * (1.0 / log2e)], axis=0)[None]
    if has_prior:
        total = total + prior[0:1]
    dg_ref[...] = jnp.broadcast_to(total, dg_ref.shape)
    for copy in copies:
        copy.wait()


def in_vmem(array):
    return pltpu.with_memory_space_constraint(array, pltpu.VMEM)


def attend(first, heads, heads_local, copies, places, facts, gains, blocks, prior, grads):
    shards = len(blocks)
    length = blocks[0].shape[1] * shards
    whole, anywhere = pl.BlockSpec(memory_space=pltpu.VMEM), pl.BlockSpec(memory_space=pl.ANY)
    grad_shape = jax.ShapeDtypeStruct((1, length, heads_local * HEAD), jnp.bfloat16)
    inputs = [*facts, gains, *[in_vmem(b) for b in blocks]] + ([] if prior is None else [prior])
    out = pl.pallas_call(
        functools.partial(attend_kernel, first, places, prior is not None),
        out_shape=[grad_shape] * 3 + [jax.ShapeDtypeStruct((copies, 2, HEAD), jnp.float32)],
        in_specs=[whole] * len(inputs) + [anywhere] * len(grads),
        out_specs=[anywhere] * 3 + [whole],
        scratch_shapes=[pltpu.VMEM((length, heads * HEAD), jnp.bfloat16)] * 3
        + [pltpu.VMEM((heads, length, length), jnp.bfloat16)] * 2
        + [pltpu.SemaphoreType.DMA((3 * heads,))],
        input_output_aliases={len(inputs) + i: i for i in range(len(grads))},
        cost_estimate=pl.CostEstimate(
            flops=heads * 12 * length * length * HEAD,
            bytes_accessed=heads * 8 * length * HEAD * 2,
            transcendentals=heads * length * length,
        ),
        name="attend",
    )(*inputs, *grads)
    return out[:3], out[3]


AXES = ("segment", "dp", "seq")


def gathered_sum(value, groups):
    if value.shape[0] == 1:
        value = jnp.broadcast_to(value, (len(groups[0]), *value.shape[1:]))
    arrived = lax.all_to_all(value, AXES, 0, 0, tiled=True, axis_index_groups=groups)
    return jnp.sum(arrived, axis=0, keepdims=True)


def gain_groups():
    segments, replicas, shards = (lax.axis_size(a) for a in AXES)
    fast = 2 if replicas % 2 == 0 else 1
    slow = replicas // fast

    def index(s, z, y, q):
        return (s * replicas + z * fast + y) * shards + q

    near = [(s, y, q) for s in range(segments) for y in range(fast) for q in range(shards)]
    planes = [[index(s, z, y, q) for s, y, q in near] for z in range(slow)]
    lines = [[index(s, z, y, q) for z in range(slow)] for s, y, q in near]
    return planes, lines


def body(
    query_in,
    key_in,
    value_in,
    latent_now,
    latent_next,
    norm_gains,
    rewards,
    step_index,
    token_count,
):
    segments = lax.axis_size("segment")
    replicas = lax.axis_size("dp")
    shards = lax.axis_size("seq")
    heads_local = query_in.shape[2] // HEAD // shards
    chunks = chunks_of(heads_local)

    plan = [(STAY, 0, heads_local)]
    for first, heads in chunks:
        plan += [(steps, first, heads) for steps in (SAME, BACK, FAR)]
    sent = pack(plan, shards, (query_in, key_in, value_in, latent_now, latent_next))
    arrived = {(steps, first): moved(a, steps) for (steps, first, _), a in zip(plan, sent)}

    facts = tuple(a[None] for a in (rewards, step_index, token_count))
    grads, partial = (), None
    places = (STAY, SAME, BACK, FAR)
    for c, (first, heads) in enumerate(chunks):
        blocks = [arrived[STAY, 0]] + [arrived[steps, first] for steps in places[1:]]
        copies = segments * shards * 2 if c == len(chunks) - 1 else 1
        grads, partial = attend(
            first, heads, heads_local, copies, places, facts, norm_gains, blocks, partial, grads
        )
    planes, lines = gain_groups()
    total = gathered_sum(gathered_sum(partial, planes), lines)[0]
    return (*grads, total / (segments * replicas))


def solution(mesh):
    rows = P(("segment", "dp"), "seq", None)
    return jax.shard_map(
        body,
        mesh=mesh,
        in_specs=(rows,) * 5 + (P(),) * 4,
        out_specs=(P(("segment", "dp"), None, "seq"),) * 3 + (P(),),
        check_vma=False,
    )
```

```python
import functools
import math

import jax
import jax.numpy as jnp
from jax import lax
from jax.experimental import pallas as pl
from jax.experimental.pallas import tpu as pltpu
from jax.sharding import PartitionSpec as P

HEAD = 128
STEPS = 16
GROUP = 16
STAY, SAME, FAR, BACK = (0, 0), (-1, 1), (2, 2), (1, -1)


def chunks_of(heads):
    return ((0, heads - 1), (heads - 1, 1)) if heads > 1 else ((0, 1),)


def step_at(steps, replica, shards):
    return jnp.where(replica % 2 == 0, steps[0] % shards, steps[1] % shards)


def moved(value, steps):
    segments, replicas, shards = (lax.axis_size(a) for a in ("segment", "dp", "seq"))
    pairs = []
    for s in range(segments):
        for r in range(replicas):
            for q in range(shards):
                to = (q + steps[r % 2]) % shards
                pairs.append(
                    ((s * replicas + r) * shards + q, ((s + 1) % segments * replicas + r) * shards + to)
                )
    return lax.ppermute(value, ("segment", "dp", "seq"), pairs)


def pack_kernel(plan, shards, query, key, value, now, following, *rest):
    outs, (now_ref, next_ref, sems) = rest[: len(plan)], rest[len(plan) :]
    mine, replica = lax.axis_index("seq"), lax.axis_index("dp")
    width = query.shape[2] // shards
    late = [
        pltpu.make_async_copy(now.at[0], now_ref, sems.at[0]),
        pltpu.make_async_copy(following.at[0], next_ref, sems.at[1]),
    ]
    for copy in late:
        copy.start()
    places, copies = [], []
    for n, ((steps, first, heads), out) in enumerate(zip(plan, outs)):
        place = lax.rem(mine + step_at(steps, replica, shards), shards) * width + first * HEAD
        cols = pl.ds(pl.multiple_of(place, HEAD), heads * HEAD)
        places.append(cols)
        for at, array in enumerate((query, key, value)):
            copy = pltpu.make_async_copy(array.at[0, :, cols], out.at[at], sems.at[2 + 3 * n + at])
            copy.start()
            copies.append(copy)
    for copy in late:
        copy.wait()
    for cols, out in zip(places, outs):
        out[3] = (
            next_ref[:, cols].astype(jnp.float32) - now_ref[:, cols].astype(jnp.float32)
        ).astype(jnp.bfloat16)
    for copy in copies:
        copy.wait()


def pack(plan, shards, arrays):
    _, rows, width = arrays[0].shape
    return pl.pallas_call(
        functools.partial(pack_kernel, plan, shards),
        out_shape=[pltpu.VMEM((4, rows, heads * HEAD), jnp.bfloat16) for _, _, heads in plan],
        in_specs=[pl.BlockSpec(memory_space=pl.ANY)] * 5,
        out_specs=[pl.BlockSpec(memory_space=pltpu.VMEM)] * len(plan),
        scratch_shapes=[pltpu.VMEM((rows, width), jnp.bfloat16)] * 2
        + [pltpu.SemaphoreType.DMA((2 + 3 * len(plan),))],
        cost_estimate=pl.CostEstimate(flops=1, bytes_accessed=2 << 20, transcendentals=0),
        name="pack",
    )(*arrays)


def slot_scalars(source, rewards, steps, counts):
    total = rewards.shape[1]
    lane = lax.broadcasted_iota(jnp.int32, (1, total), 1)
    of_group = (lane // GROUP) == (source // GROUP)
    of_slot = lane == source

    def picked(which, row):
        return jnp.sum(jnp.where(which, row, jnp.zeros_like(row)), axis=1, keepdims=True)

    mean = picked(of_group, rewards) / GROUP
    spread = jnp.sqrt(picked(of_group, (rewards - mean) ** 2) / GROUP)
    advantage = (picked(of_slot, rewards) - mean) / jnp.maximum(spread, jnp.float32(0.25))
    index = picked(of_slot, steps.astype(jnp.float32))

    def sigma(k):
        level = 1.0 - k / STEPS
        return 7.0 * level / (1.0 + 6.0 * level)

    delta = sigma(index) - sigma(index + 1.0)
    count = picked(of_slot, counts.astype(jnp.float32))
    return advantage, delta, count


def dot(a, b, dims):
    return lax.dot_general(a, b, (dims, ((), ())), preferred_element_type=jnp.float32)


def attend_kernel(first, places, has_prior, rewards, steps, counts, gains, *rest):
    blocks, rest = rest[: len(places)], rest[len(places) :]
    prior = rest[0] if has_prior else None
    dq_hbm, dk_hbm, dv_hbm, dg_ref, dq_ref, dk_ref, dv_ref, e_ref, ds_ref, sems = rest[-10:]
    mine, replica = lax.axis_index("seq"), lax.axis_index("dp")
    segments, replicas = lax.axis_size("segment"), lax.axis_size("dp")
    source = lax.rem(lax.axis_index("segment") + segments - 1, segments) * replicas + replica
    advantage, delta, count = slot_scalars(source, rewards[...], steps[...], counts[...])
    shards, rows = len(blocks), blocks[0].shape[1]
    heads = dq_ref.shape[1] // HEAD
    each = [(h, d) for h in range(heads) for d in range(shards)]
    gain_q, gain_k = gains[0:1, :], gains[1:2, :]
    inv_root = 1.0 / math.sqrt(HEAD)
    log2e = math.log2(math.e)
    starts, alive = [], []
    for place in places:
        start = lax.rem(mine - step_at(place, replica, shards) + shards, shards) * rows
        starts.append(pl.multiple_of(start, rows))
        token = lax.broadcasted_iota(jnp.int32, (rows, HEAD), 0) + start
        alive.append(jnp.where(token.astype(jnp.float32) < count, jnp.float32(1.0), 0.0))
    alive_low = [a.astype(jnp.bfloat16) for a in alive]
    keep = jnp.concatenate(alive_low, axis=0)

    def part(h, d, at):
        block = blocks[d]
        skip = first * HEAD if block.shape[2] > dq_ref.shape[1] else 0
        return block[at, :, skip + h * HEAD : skip + (h + 1) * HEAD]

    def normed(h, d, at):
        wide = part(h, d, at).astype(jnp.float32)
        scale = lax.rsqrt(jnp.mean(wide * wide, axis=-1, keepdims=True) + 1e-06)
        if at == 1:
            scale = scale * alive[d]
        return wide * scale, scale

    def stack(piece, h):
        return jnp.concatenate([piece[h, d] for d in range(shards)], axis=0)

    def cols(h):
        return slice(h * HEAD, (h + 1) * HEAD)

    copies = []

    def give(kind, staged, hbm, h):
        copy = pltpu.make_async_copy(
            staged.at[:, cols(h)],
            hbm.at[0, :, pl.ds((first + h) * HEAD, HEAD)],
            sems.at[3 * h + kind],
        )
        copy.start()
        copies.append(copy)

    q_hat, q_scale, q_rows, k_hat, k_scale, k_rows, v_rows = ({} for _ in range(7))
    for h, d in each:
        k_hat[h, d], k_scale[h, d] = normed(h, d, 1)
        k_rows[h, d] = (k_hat[h, d] * gain_k).astype(jnp.bfloat16)
    for h, d in each:
        q_hat[h, d], q_scale[h, d] = normed(h, d, 0)
        q_rows[h, d] = (q_hat[h, d] * (gain_q * (inv_root * log2e))).astype(jnp.bfloat16)
        v_rows[h, d] = part(h, d, 2) * alive_low[d]
    keys = [stack(k_rows, h) for h in range(heads)]
    values = [stack(v_rows, h) for h in range(heads)]

    e = {}
    for h, d in each:
        e[h, d] = jnp.exp2(dot(q_rows[h, d], keys[h], ((1,), (1,)))).astype(jnp.bfloat16)
        e_ref[h, d * rows : (d + 1) * rows, :] = e[h, d]
    pull, level = {}, {}
    for h, d in each:
        both = dot(e[h, d], jnp.concatenate([values[h], keep], axis=1), ((1,), (0,)))
        share = 1.0 / both[:, HEAD:]
        velocity = both[:, :HEAD] * share
        change = part(h, d, 3).astype(jnp.float32) + delta * velocity
        pull[h, d] = (change * (share * (alive[d] * advantage))).astype(jnp.bfloat16)
        level[h, d] = jnp.sum(
            pull[h, d].astype(jnp.float32) * velocity, axis=-1, keepdims=True
        )
    ds = {}
    for h, d in each:
        d_weights = dot(pull[h, d], values[h], ((1,), (1,)))
        ds[h, d] = e_ref[h, d * rows : (d + 1) * rows, :] * (d_weights - level[h, d]).astype(
            jnp.bfloat16
        )
        ds_ref[h, d * rows : (d + 1) * rows, :] = ds[h, d]
    d_values = [dot(e_ref[h], stack(pull, h), ((0,), (0,))) for h in range(heads)]
    d_queries = {}
    for h, d in each:
        d_queries[h, d] = dot(ds[h, d], keys[h], ((1,), (0,)))
    d_keys = [dot(ds_ref[h], stack(q_rows, h), ((0,), (0,))) for h in range(heads)]

    def unnormed(d_rows, hat, scale, gain):
        shared = d_rows * hat
        inner = d_rows * gain - hat * jnp.mean(shared * gain, axis=-1, keepdims=True)
        return (inner * scale).astype(jnp.bfloat16), jnp.sum(shared, axis=0, keepdims=True)

    for h in range(heads):
        for d in range(shards):
            d_rows = d_values[h][d * rows : (d + 1) * rows].astype(jnp.bfloat16) * alive_low[d]
            dv_ref[pl.ds(starts[d], rows), cols(h)] = d_rows
        give(2, dv_ref, dv_hbm, h)
    grad_gq = jnp.zeros((1, HEAD), jnp.float32)
    for h in range(heads):
        for d in range(shards):
            out, summed = unnormed(d_queries[h, d], q_hat[h, d], q_scale[h, d], gain_q * inv_root)
            dq_ref[pl.ds(starts[d], rows), cols(h)] = out
            grad_gq += summed
        give(0, dq_ref, dq_hbm, h)
    grad_gk = jnp.zeros((1, HEAD), jnp.float32)
    for h in range(heads):
        for d in range(shards):
            d_rows = d_keys[h][d * rows : (d + 1) * rows]
            out, summed = unnormed(d_rows, k_hat[h, d], k_scale[h, d], gain_k * (1.0 / log2e))
            dk_ref[pl.ds(starts[d], rows), cols(h)] = out
            grad_gk += summed
        give(1, dk_ref, dk_hbm, h)
    total = jnp.concatenate([grad_gq * inv_root, grad_gk * (1.0 / log2e)], axis=0)[None]
    if has_prior:
        total = total + prior[0:1]
    dg_ref[...] = jnp.broadcast_to(total, dg_ref.shape)
    for copy in copies:
        copy.wait()


def in_vmem(array):
    return pltpu.with_memory_space_constraint(array, pltpu.VMEM)


def attend(first, heads, heads_local, copies, places, facts, gains, blocks, prior, grads):
    shards = len(blocks)
    length = blocks[0].shape[1] * shards
    whole, anywhere = pl.BlockSpec(memory_space=pltpu.VMEM), pl.BlockSpec(memory_space=pl.ANY)
    grad_shape = jax.ShapeDtypeStruct((1, length, heads_local * HEAD), jnp.bfloat16)
    inputs = [in_vmem(a) for a in (*facts, gains, *blocks, *(() if prior is None else (prior,)))]
    out = pl.pallas_call(
        functools.partial(attend_kernel, first, places, prior is not None),
        out_shape=[grad_shape] * 3 + [pltpu.VMEM((copies, 2, HEAD), jnp.float32)],
        in_specs=[whole] * len(inputs) + [anywhere] * len(grads),
        out_specs=[anywhere] * 3 + [whole],
        scratch_shapes=[pltpu.VMEM((length, heads * HEAD), jnp.bfloat16)] * 3
        + [pltpu.VMEM((heads, length, length), jnp.bfloat16)] * 2
        + [pltpu.SemaphoreType.DMA((3 * heads,))],
        input_output_aliases={len(inputs) + i: i for i in range(len(grads))},
        cost_estimate=pl.CostEstimate(
            flops=heads * 12 * length * length * HEAD,
            bytes_accessed=heads * 8 * length * HEAD * 2,
            transcendentals=heads * length * length,
        ),
        name="attend",
    )(*inputs, *grads)
    return out[:3], out[3]


AXES = ("segment", "dp", "seq")


def gathered_sum(value, groups):
    if value.shape[0] == 1:
        value = jnp.broadcast_to(value, (len(groups[0]), *value.shape[1:]))
    arrived = lax.all_to_all(value, AXES, 0, 0, tiled=True, axis_index_groups=groups)
    return jnp.sum(arrived, axis=0, keepdims=True)


def gain_groups():
    segments, replicas, shards = (lax.axis_size(a) for a in AXES)
    fast = 2 if replicas % 2 == 0 else 1
    slow = replicas // fast

    def index(s, z, y, q):
        return (s * replicas + z * fast + y) * shards + q

    near = [(s, y, q) for s in range(segments) for y in range(fast) for q in range(shards)]
    planes = [[index(s, z, y, q) for s, y, q in near] for z in range(slow)]
    lines = [[index(s, z, y, q) for z in range(slow)] for s, y, q in near]
    return planes, lines


def body(
    query_in,
    key_in,
    value_in,
    latent_now,
    latent_next,
    norm_gains,
    rewards,
    step_index,
    token_count,
):
    segments = lax.axis_size("segment")
    replicas = lax.axis_size("dp")
    shards = lax.axis_size("seq")
    heads_local = query_in.shape[2] // HEAD // shards
    chunks = chunks_of(heads_local)

    plan = [(STAY, 0, heads_local)]
    for first, heads in chunks:
        plan += [(steps, first, heads) for steps in (SAME, BACK, FAR)]
    sent = pack(plan, shards, (query_in, key_in, value_in, latent_now, latent_next))
    arrived = {(steps, first): moved(a, steps) for (steps, first, _), a in zip(plan, sent)}

    facts = tuple(a[None] for a in (rewards, step_index, token_count))
    grads, partial = (), None
    places = (STAY, SAME, BACK, FAR)
    for c, (first, heads) in enumerate(chunks):
        blocks = [arrived[STAY, 0]] + [arrived[steps, first] for steps in places[1:]]
        copies = segments * shards * 2 if c == len(chunks) - 1 else 1
        grads, partial = attend(
            first, heads, heads_local, copies, places, facts, norm_gains, blocks, partial, grads
        )
    planes, lines = gain_groups()
    total = gathered_sum(gathered_sum(partial, planes), lines)[0]
    return (*grads, total / (segments * replicas))


def solution(mesh):
    rows = P(("segment", "dp"), "seq", None)
    return jax.shard_map(
        body,
        mesh=mesh,
        in_specs=(rows,) * 5 + (P(),) * 4,
        out_specs=(P(("segment", "dp"), None, "seq"),) * 3 + (P(),),
        check_vma=False,
    )
```
